32 devices in a mesh: store: 8 (over y, x, core), vocab: 4 (over z).
Axes of the slice: x: 2, y: 2, z: 4, core: 2. Of those that a mesh axis runs over, the one named last changes fastest.
Arguments:
- hidden: bfloat16 [512, 4096], P('store')
- lm_head: bfloat16 [4096, 65536], P(None, ('store', 'vocab'))
- store_keys: bfloat16 [8192, 4096], P(('store', 'vocab'))
- values: int32 [8192], P(('store', 'vocab')), may hold values from 0 to 65535, as said below
- licences: int32 [8192], P(('store', 'vocab')), may hold values from 0 to 29, as said below
- allowed: int32 [512], replicated, may hold values from 1 to 1073741823, as said below
Outputs:
- log_probs: float32 [512, 65536], P(None, ('store', 'vocab'))
The draws below stay inside these ranges and needn't reach their ends.
Inputs may be any that keep to these rules, and one draw needn't show every extreme that they name: `values`: entry i holds a token t with t // 2048 = (i // 1024) * 4 + (i // 64) % 4: the entries of a device name tokens of the 8192 columns of its index along store, and its k-th run of 64 entries names tokens of the k-th 2048 columns of those. `licences`: some entry has licence 0. `allowed`: bit l of a position's word says whether licence l may be used; bit 0 is always set.
All inputs are finite; a program needn't handle non-finite values.
Results may differ from the reference program's by a relative error of at most 0.0003.
Values may be sent and summed in bfloat16 or wider, within the bound.
A program may use at most 128 MiB of HBM per device.

```python
import math
import jax
import jax.numpy as jnp
from jax import lax

D = 4096
VOCAB = 65536
QUERIES = 512
ENT_DEV = 256
NLIC = 30
ENTRIES = 8192
SLAB_COLS = 8192
OWN_COLS = 2048
BLOCK = 64


def key_row(key, index):
    row_key = jax.random.fold_in(jax.random.fold_in(key, 101), index)
    entries = jnp.clip(jax.random.normal(row_key, (D,), jnp.float32), -6.0, 6.0)
    shrink = 1.0 - 0.02 * index.astype(jnp.float32) / ENTRIES
    return entries * shrink


def head_column(key, column):
    column_key = jax.random.fold_in(jax.random.fold_in(key, 202), column)
    entries = jnp.clip(jax.random.normal(column_key, (D,), jnp.float32), -6.0, 6.0)
    growth = 3.5 * (0.8 + 0.4 * column.astype(jnp.float32) / VOCAB) / math.sqrt(D)
    return entries * growth


def draw_store_keys(key, part):
    rows = jax.vmap(lambda index: key_row(key, index))(jnp.arange(ENTRIES, dtype=jnp.int32))
    return rows.astype(jnp.bfloat16)


def draw_lm_head(key, part):
    columns = jax.vmap(lambda column: head_column(key, column))(jnp.arange(VOCAB, dtype=jnp.int32)).T
    return columns.astype(jnp.bfloat16)


def draw_hidden(key, part):
    base_key = jax.random.fold_in(key, 303)
    return jnp.clip(jax.random.normal(base_key, (QUERIES, D), jnp.float32), -6.0, 6.0).astype(jnp.bfloat16)


def draw_values(key, part):
    index = jnp.arange(ENTRIES, dtype=jnp.int32)
    per_slab = SLAB_COLS // OWN_COLS
    slab_index = index // (ENT_DEV * per_slab)
    within = index // BLOCK % per_slab
    offset = jax.random.randint(jax.random.fold_in(key, 7), (ENTRIES,), 0, OWN_COLS)
    offset = jnp.where(index == 0, 0, offset)
    offset = jnp.where(index == ENTRIES - 1, OWN_COLS - 1, offset)
    return ((slab_index * per_slab + within) * OWN_COLS + offset).astype(jnp.int32)


def draw_licences(key, part):
    index = jnp.arange(ENTRIES, dtype=jnp.int32)
    drawn = jax.random.randint(jax.random.fold_in(key, 8), (ENTRIES,), 0, NLIC)
    drawn = jnp.where(index == 0, 0, drawn)
    return jnp.where(index == 1, NLIC - 1, drawn).astype(jnp.int32)


def draw_allowed(key, part):
    index = jnp.arange(QUERIES, dtype=jnp.int32)
    words = jax.random.randint(jax.random.fold_in(key, 9), (QUERIES,), 0, 2 ** 30)
    words = jnp.bitwise_or(words, 1)
    words = jnp.where(index == 0, 2 ** 30 - 1, words)
    return jnp.where(index == 1, 1, words).astype(jnp.int32)


def setup_inputs(seed: int = 0) -> dict:
    key_of = jax.random.split(jax.random.key(seed), 7)
    return {
        "hidden": draw_hidden(jax.random.fold_in(key_of[6], 71), 0),
        "lm_head": draw_lm_head(jax.random.fold_in(key_of[6], 71), 0),
        "store_keys": draw_store_keys(jax.random.fold_in(key_of[6], 71), 0),
        "values": draw_values(jax.random.fold_in(key_of[6], 71), 0),
        "licences": draw_licences(jax.random.fold_in(key_of[6], 71), 0),
        "allowed": draw_allowed(jax.random.fold_in(key_of[6], 71), 0),
    }


NEG_FILL = -1e+30

def half_norm(block_rows):
    wide = block_rows.astype(jnp.float32)
    return 0.5 * lax.optimization_barrier(jnp.sum(wide * wide, axis=1)) / math.sqrt(D)

def reference(hidden, lm_head, store_keys, values, licences, allowed):
    logits = jnp.dot(hidden, lm_head, preferred_element_type=jnp.float32)
    lm_max = lax.optimization_barrier(jnp.max(logits, axis=1, keepdims=True))
    lm_total = lax.optimization_barrier(jnp.sum(jnp.exp(logits - lm_max), axis=1, keepdims=True))
    lm_log = logits - lm_max - jnp.log(lm_total)
    key_half = lax.map(half_norm, store_keys.reshape(-1, ENT_DEV, D)).reshape(-1)
    products = lax.dot_general(hidden, store_keys, (((1,), (1,)), ((), ())), preferred_element_type=jnp.float32)
    scores = products / math.sqrt(D) - key_half[None, :]
    permitted = jnp.bitwise_and(jnp.right_shift(allowed[:, None], licences[None, :]), 1) == 1
    masked = jnp.where(permitted, scores, NEG_FILL)
    knn_max = lax.optimization_barrier(jnp.max(masked, axis=1, keepdims=True))
    kernel = jnp.where(permitted, jnp.exp(masked - knn_max), 0.0)
    knn_total = lax.optimization_barrier(jnp.sum(kernel, axis=1, keepdims=True))
    knn_mass = jnp.zeros((QUERIES, VOCAB), jnp.float32).at[:, values].add(kernel)
    share = knn_mass / knn_total
    present = share > 0.0
    knn_log = jnp.where(present, jnp.log(jnp.where(present, share, 1.0)), -jnp.inf)
    return jnp.logaddexp(math.log(0.75) + lm_log, math.log(0.25) + knn_log)
```

```python
import functools
import math

import jax
import jax.numpy as jnp
from jax import lax
from jax.experimental import pallas as pl
from jax.experimental.pallas import tpu as pltpu
from jax.sharding import PartitionSpec as P

NEG_FILL = -1e30
DEPTH_CHUNK = 512
MESH = pl.DeviceIdType.MESH


def row_to_column(row, lanes=128):
    return jnp.broadcast_to(row, (lanes, row.shape[1])).T


def gather_kernel(
    S, V,
    hidden, lm_head, keys, values, licences, allowed,
    logits_out, weights_out, tokens_out, shift_out,
    hid, head, key, logits, scores, half, wsend, wrecv, tok, tokcol, turn, stat, st1, st1_all, st2, st2_all,
    own_sem, head_sem, key_sem, out_sem, gsend, grecv, tsend, trecv, wsend_sem, wrecv_sem,
    s1send, s1recv, s2send, s2recv,
):
    R, D = hidden.shape
    C = lm_head.shape[1]
    E = keys.shape[0]
    Q = hid.shape[1]
    K, KC = hid.shape[0], hid.shape[2]
    B = E // V
    inverse_root = 1.0 / math.sqrt(D)
    s = lax.axis_index("store")
    v = lax.axis_index("vocab")

    def rows(origin):
        return pl.ds(pl.multiple_of(origin * R, R), R)

    def remote(src, dst, send, recv, store, vocab):
        return pltpu.make_async_remote_copy(
            src_ref=src, dst_ref=dst, send_sem=send, recv_sem=recv,
            device_id=(store, vocab), device_id_type=MESH,
        )

    def own_copy(k):
        return pltpu.make_async_copy(
            hidden.at[:, pl.ds(pl.multiple_of(k * KC, KC), KC)], hid.at[k, rows(s)], own_sem.at[k]
        )

    def head_copy(k):
        return pltpu.make_async_copy(
            lm_head.at[pl.ds(pl.multiple_of(k * KC, KC), KC)], head.at[k], head_sem.at[k]
        )

    def key_copy(k):
        return pltpu.make_async_copy(
            keys.at[:, pl.ds(pl.multiple_of(k * KC, KC), KC)], key.at[k], key_sem.at[k]
        )

    def loop_all(f):
        def step(k, carry):
            f(k)
            return carry
        lax.fori_loop(0, K, step, 0)

    loop_all(lambda k: own_copy(k).start())
    loop_all(lambda k: key_copy(k).start())
    tok[...] = jnp.broadcast_to(values[...], tok.shape)

    store_peers = [lax.rem(s + j, S) for j in range(1, S)]
    vocab_peers = [lax.rem(v + j, V) for j in range(1, V)]
    vocab_from = [lax.rem(v + V - j, V) for j in range(1, V)]
    store_from = [lax.rem(s + S - j, S) for j in range(1, S)]

    barrier = pltpu.get_barrier_semaphore()
    for peer in store_peers:
        pl.semaphore_signal(barrier, inc=1, device_id=(peer, v), device_id_type=MESH)
    for peer in vocab_peers:
        pl.semaphore_signal(barrier, inc=1, device_id=(s, peer), device_id_type=MESH)
    pl.semaphore_wait(barrier, S + V - 2)

    tuned = S == 8 and V % 2 == 0
    if tuned:
        odd = lax.rem(v, 2)
        along_x = 2 - 4 * lax.rem(lax.div(s, 2), 2)
        along_y = 4 - 8 * lax.rem(lax.div(s, 4), 2)
        first = s + along_x * (1 - odd) + along_y * odd
        second = s + along_y * (1 - odd) + along_x * odd
        diagonal = s + along_x + along_y
        across = 1 - 2 * lax.rem(s, 2)
        pair = v + 1 - 2 * odd
        streams = [
            (s, (first, v), first),
            (first, (second, v), diagonal),
            (first, (s, pair), second),
            (s, (s + across, v), s + across),
            (first, (s + across, v), first + across),
            (diagonal, (s + across, v), diagonal + across),
            (second, (s + across, v), second + across),
        ]
    else:
        streams = [(s, (peer, v), source) for peer, source in zip(store_peers, store_from)]

    def send(t, k):
        origin, target, _ = streams[t]
        if origin is s:
            src = hidden.at[:, pl.ds(pl.multiple_of(k * KC, KC), KC)]
        else:
            src = hid.at[k, rows(origin)]
        return remote(src, hid.at[k, rows(origin)], gsend.at[t, k], grecv.at[t, k], *target)

    def arrive(t, k):
        _, target, origin = streams[t]
        block = hid.at[k, rows(origin)]
        return remote(block, block, gsend.at[t, k], grecv.at[t, k], *target)

    if tuned:
        loop_all(lambda k: send(0, k).start())
        loop_all(lambda k: send(3, k).start())
    else:
        for t in range(len(streams)):
            loop_all(lambda k: send(t, k).start())
    loop_all(lambda k: head_copy(k).start())

    token_sends = []
    for j in range(1, V):
        copy = remote(tok, tokcol.at[v], tsend.at[j - 1], trecv.at[j - 1], s, vocab_peers[j - 1])
        copy.start()
        token_sends.append(copy)
    tokcol[v] = tok[...]

    logits[...] = jnp.zeros_like(logits)
    scores[...] = jnp.zeros_like(scores)
    half[...] = jnp.zeros_like(half)

    def norm_step(k, carry):
        key_copy(k).wait()
        wide = key[k].astype(jnp.float32)
        half[...] += jnp.sum(wide * wide, axis=1, keepdims=True)
        return carry

    lax.fori_loop(0, K, norm_step, 0)

    NT = math.gcd(C, 256)

    def compute(k):
        own_copy(k).wait()
        scores[...] += lax.dot_general(
            key[k], hid[k], (((1,), (1,)), ((), ())), preferred_element_type=jnp.float32
        )
        head_copy(k).wait()

        def column_step(n, carry):
            cols = pl.ds(pl.multiple_of(n * NT, NT), NT)
            logits[:, cols] += jnp.dot(
                hid[k], head[k, :, cols], preferred_element_type=jnp.float32
            )
            return carry

        lax.fori_loop(0, C // NT, column_step, 0)

    if tuned:
        def gather_step(k, carry):
            @pl.when(k < K)
            def _():
                arrive(0, k).wait_recv()
                send(1, k).start()
                send(2, k).start()
                send(4, k).start()

            @pl.when(jnp.logical_and(k >= 1, k <= K))
            def _():
                arrive(1, k - 1).wait_recv()
                send(5, k - 1).start()
                arrive(2, k - 1).wait_recv()
                send(6, k - 1).start()

            @pl.when(k >= 2)
            def _():
                for t in range(3, 7):
                    arrive(t, k - 2).wait_recv()
                compute(k - 2)

            return carry

        lax.fori_loop(0, K + 2, gather_step, 0)
    else:
        def gather_step(k, carry):
            for t in range(len(streams)):
                arrive(t, k).wait_recv()
            compute(k)
            return carry

        lax.fori_loop(0, K, gather_step, 0)

    out_copy = pltpu.make_async_copy(logits, logits_out, out_sem)
    out_copy.start()

    licence = row_to_column(licences[...])[:, 0:1]
    permitted = jnp.bitwise_and(
        jnp.right_shift(
            jnp.broadcast_to(allowed[...], (E, Q)), jnp.broadcast_to(licence, (E, Q))
        ), 1) == 1
    masked = jnp.where(
        permitted, scores[...] * inverse_root - (0.5 * inverse_root) * half[...], NEG_FILL
    )
    near = jnp.max(masked, axis=0, keepdims=True)
    kernel = jnp.where(permitted, jnp.exp(masked - near), 0.0)
    mass = jnp.sum(kernel, axis=0, keepdims=True)
    wsend[...] = kernel.astype(jnp.bfloat16)
    weight_sends = []
    for j in range(1, V):
        peer = vocab_peers[j - 1]
        copy = remote(
            wsend.at[pl.ds(pl.multiple_of(peer * B, B), B)], wrecv.at[v],
            wsend_sem.at[j - 1], wrecv_sem.at[j - 1], s, peer,
        )
        copy.start()
        weight_sends.append(copy)
    wrecv[v] = wsend[pl.ds(pl.multiple_of(v * B, B), B), :]

    RT = math.gcd(Q, 64)
    lane = lax.broadcasted_iota(jnp.int32, (RT, 128), 1)

    def stat_step(r, carry):
        span = pl.ds(pl.multiple_of(r * RT, RT), RT)
        tile = logits[span, :]
        top = jnp.max(tile, axis=1, keepdims=True)
        total = jnp.sum(jnp.exp(tile - top), axis=1, keepdims=True)
        stat[span, :] = jnp.where(
            lane == 0, jnp.broadcast_to(top, (RT, 128)), jnp.broadcast_to(total, (RT, 128))
        )
        return carry

    lax.fori_loop(0, Q // RT, stat_step, 0)
    st1[0:2, :] = stat[...].T[0:2, :]
    st1[2:3, :] = near
    st1[3:4, :] = mass
    st1[4:8, :] = jnp.zeros((4, Q), jnp.float32)
    stat_sends = []
    for j in range(1, S):
        copy = remote(st1, st1_all.at[s], s1send.at[j - 1], s1recv.at[j - 1], store_peers[j - 1], v)
        copy.start()
        stat_sends.append(copy)
    st1_all[s] = st1[...]

    first_col = (s * V + v) * C
    for j in range(1, V):
        slot = tokcol.at[vocab_from[j - 1]]
        remote(slot, slot, tsend.at[j - 1], trecv.at[j - 1], s, vocab_peers[j - 1]).wait_recv()
    for u in range(V):
        turn[...] = row_to_column(tokcol[u, 0:1, :])
        tokens_out[u * B:(u + 1) * B, :] = turn[pl.ds(pl.multiple_of(v * B, B), B), :] - first_col

    def merge(ref, n):
        top = ref[0, 0:1, :]
        near_top = ref[0, 2:3, :]
        for i in range(1, n):
            top = jnp.maximum(top, ref[i, 0:1, :])
            near_top = jnp.maximum(near_top, ref[i, 2:3, :])
        total = jnp.zeros_like(top)
        near_total = jnp.zeros_like(top)
        for i in range(n):
            total += ref[i, 1:2, :] * jnp.exp(ref[i, 0:1, :] - top)
            near_total += ref[i, 3:4, :] * jnp.exp(ref[i, 2:3, :] - near_top)
        return top, total, near_top, near_total

    for j in range(1, S):
        slot = st1_all.at[store_from[j - 1]]
        remote(slot, slot, s1send.at[j - 1], s1recv.at[j - 1], store_peers[j - 1], v).wait_recv()
    for i, row in enumerate(merge(st1_all, S)):
        st2[i:i + 1, :] = row
    st2[4:5, :] = near
    st2[5:8, :] = jnp.zeros((3, Q), jnp.float32)
    for j in range(1, V):
        copy = remote(st2, st2_all.at[v], s2send.at[j - 1], s2recv.at[j - 1], s, vocab_peers[j - 1])
        copy.start()
        stat_sends.append(copy)
    st2_all[v] = st2[...]
    for j in range(1, V):
        source = vocab_from[j - 1]
        slot = st2_all.at[source]
        remote(slot, slot, s2send.at[j - 1], s2recv.at[j - 1], s, vocab_peers[j - 1]).wait_recv()
        slot = wrecv.at[source]
        remote(slot, slot, wsend_sem.at[j - 1], wrecv_sem.at[j - 1], s, vocab_peers[j - 1]).wait_recv()
    top, total, near_top, near_total = merge(st2_all, V)
    shift_out[...] = row_to_column(top + jnp.log(total) - math.log(0.75))
    for u in range(V):
        scale = 0.25 * jnp.exp(st2_all[u, 4:5, :] - near_top) / near_total
        weights_out[u * B:(u + 1) * B, :] = (wrecv[u].astype(jnp.float32) * scale).astype(jnp.bfloat16)

    if tuned:
        def drain(k):
            for t in range(len(streams)):
                send(t, k).wait_send()
        loop_all(drain)
    else:
        for t in range(len(streams)):
            loop_all(lambda k: send(t, k).wait_send())
    for copy in token_sends + weight_sends + stat_sends:
        copy.wait_send()
    out_copy.wait()


def mixture_kernel(weights, tokens, shift, logits, out):
    columns = lax.broadcasted_iota(jnp.int32, (tokens.shape[0], out.shape[1]), 1)
    columns += pl.program_id(0) * out.shape[1]
    table = jnp.where(tokens[:, 0:1] == columns, 1.0, 0.0).astype(jnp.bfloat16)
    share = lax.dot_general(
        weights[...], table, (((0,), (0,)), ((), ())), preferred_element_type=jnp.float32
    )
    ours = logits[...] - shift[:, 0:1]
    theirs = jnp.where(share > 0.0, jnp.log(jnp.where(share > 0.0, share, 1.0)), -jnp.inf)
    out[...] = jnp.maximum(ours, theirs) + jnp.log(1.0 + jnp.exp(-jnp.abs(ours - theirs)))


def body(S, V, hidden, lm_head, keys, values, licences, allowed):
    R, D = hidden.shape
    C = lm_head.shape[1]
    E = keys.shape[0]
    Q = allowed.shape[0]
    B = E // V
    KC = math.gcd(D, DEPTH_CHUNK)
    K = D // KC
    streams = S - 1
    any_space = pl.BlockSpec(memory_space=pl.ANY)
    vmem = pl.BlockSpec(memory_space=pltpu.VMEM)
    f32 = jnp.float32
    dma = pltpu.SemaphoreType.DMA
    logits, weights, tokens, shift = pl.pallas_call(
        functools.partial(gather_kernel, S, V),
        out_shape=(
            jax.ShapeDtypeStruct((Q, C), f32),
            jax.ShapeDtypeStruct((E, Q), jnp.bfloat16),
            jax.ShapeDtypeStruct((E, 128), jnp.int32),
            jax.ShapeDtypeStruct((Q, 128), f32),
        ),
        in_specs=[any_space] * 3 + [vmem] * 3,
        out_specs=(any_space, vmem, vmem, vmem),
        scratch_shapes=[
            pltpu.VMEM((K, Q, KC), hidden.dtype),
            pltpu.VMEM((K, KC, C), lm_head.dtype),
            pltpu.VMEM((K, E, KC), keys.dtype),
            pltpu.VMEM((Q, C), f32),
            pltpu.VMEM((E, Q), f32),
            pltpu.VMEM((E, 1), f32),
            pltpu.VMEM((E, Q), jnp.bfloat16),
            pltpu.VMEM((V, B, Q), jnp.bfloat16),
            pltpu.VMEM((8, E), jnp.int32),
            pltpu.VMEM((V, 8, E), jnp.int32),
            pltpu.VMEM((E, 128), jnp.int32),
            pltpu.VMEM((Q, 128), f32),
            pltpu.VMEM((8, Q), f32),
            pltpu.VMEM((S, 8, Q), f32),
            pltpu.VMEM((8, Q), f32),
            pltpu.VMEM((V, 8, Q), f32),
            dma((K,)), dma((K,)), dma((K,)), dma(()),
            dma((streams, K)), dma((streams, K)),
            dma((V - 1,)), dma((V - 1,)), dma((V - 1,)), dma((V - 1,)),
            dma((S - 1,)), dma((S - 1,)), dma((V - 1,)), dma((V - 1,)),
        ],
        compiler_params=pltpu.CompilerParams(
            collective_id=0, has_side_effects=True, vmem_limit_bytes=48 * 1024 * 1024
        ),
        name="gather_score",
    )(hidden, lm_head, keys, values.reshape(1, E), licences.reshape(1, E), allowed.reshape(1, Q))

    CT = math.gcd(C, 512)
    fixed = lambda shape: pl.BlockSpec(shape, lambda n: (0, 0))
    tile = pl.BlockSpec((Q, CT), lambda n: (0, n))
    return pl.pallas_call(
        mixture_kernel,
        grid=(C // CT,),
        out_shape=jax.ShapeDtypeStruct((Q, C), f32),
        in_specs=[fixed((E, Q)), fixed((E, 128)), fixed((Q, 128)), tile],
        out_specs=tile,
        compiler_params=pltpu.CompilerParams(vmem_limit_bytes=48 * 1024 * 1024),
        name="mixture",
    )(weights, tokens, shift, logits)


def solution(mesh):
    return jax.shard_map(
        functools.partial(body, mesh.shape["store"], mesh.shape["vocab"]),
        mesh=mesh,
        in_specs=(
            P("store", None),
            P(None, ("store", "vocab")),
            P(("store", "vocab"), None),
            P(("store", "vocab")),
            P(("store", "vocab")),
            P(),
        ),
        out_specs=P(None, ("store", "vocab")),
        check_vma=False,
    )
```

```python
import functools
import math

import jax
import jax.numpy as jnp
from jax import lax
from jax.experimental import pallas as pl
from jax.experimental.pallas import tpu as pltpu
from jax.sharding import PartitionSpec as P

NEG_FILL = -1e30
DEPTH_CHUNK = 1024
COLUMN_CHUNK = 1024
MESH = pl.DeviceIdType.MESH


def row_to_column(row, lanes=128):
    return jnp.broadcast_to(row, (lanes, row.shape[1])).T


def gather_kernel(
    S, V,
    hidden, lm_head, keys, values, licences, allowed,
    logits_out, weights_out, tokens_out, shift_out,
    hid, head, key, lic, allow, val, logits, scores, half, wsend, wrecv, tok, tokcol, turn, stat, st1, st1_all, st2, st2_all,
    own_sem, head_sem, key_sem, small_sem, out_sem, gsend, grecv, tsend, trecv, wsend_sem, wrecv_sem,
    s1send, s1recv, s2send, s2recv,
):
    R, D = hidden.shape
    C = lm_head.shape[1]
    E = keys.shape[0]
    Q = hid.shape[1]
    K, KC = hid.shape[0], hid.shape[2]
    B = E // V
    inverse_root = 1.0 / math.sqrt(D)
    s = lax.axis_index("store")
    v = lax.axis_index("vocab")

    def rows(origin):
        return pl.ds(pl.multiple_of(origin * R, R), R)

    def remote(src, dst, send, recv, store, vocab):
        return pltpu.make_async_remote_copy(
            src_ref=src, dst_ref=dst, send_sem=send, recv_sem=recv,
            device_id=(store, vocab), device_id_type=MESH,
        )

    def own_copy(k):
        return pltpu.make_async_copy(
            hidden.at[:, pl.ds(pl.multiple_of(k * KC, KC), KC)], hid.at[k, rows(s)], own_sem.at[k]
        )

    def head_copy(k):
        return pltpu.make_async_copy(
            lm_head.at[pl.ds(pl.multiple_of(k * KC, KC), KC)], head.at[k], head_sem.at[k]
        )

    def key_copy(k):
        return pltpu.make_async_copy(
            keys.at[:, pl.ds(pl.multiple_of(k * KC, KC), KC)], key.at[k], key_sem.at[k]
        )

    def loop_all(f):
        def step(k, carry):
            f(k)
            return carry
        lax.fori_loop(0, K, step, 0)

    loop_all(lambda k: own_copy(k).start())
    loop_all(lambda k: key_copy(k).start())
    small = [
        pltpu.make_async_copy(src, dst, small_sem.at[i])
        for i, (src, dst) in enumerate(((values, val), (licences, lic), (allowed, allow)))
    ]
    for copy in small:
        copy.start()

    store_peers = [lax.rem(s + j, S) for j in range(1, S)]
    vocab_peers = [lax.rem(v + j, V) for j in range(1, V)]
    vocab_from = [lax.rem(v + V - j, V) for j in range(1, V)]
    store_from = [lax.rem(s + S - j, S) for j in range(1, S)]

    barrier = pltpu.get_barrier_semaphore()
    for peer in store_peers:
        pl.semaphore_signal(barrier, inc=1, device_id=(peer, v), device_id_type=MESH)
    for peer in vocab_peers:
        pl.semaphore_signal(barrier, inc=1, device_id=(s, peer), device_id_type=MESH)
    pl.semaphore_wait(barrier, S + V - 2)

    tuned = S == 8 and V % 2 == 0
    if tuned:
        odd = lax.rem(v, 2)
        along_x = 2 - 4 * lax.rem(lax.div(s, 2), 2)
        along_y = 4 - 8 * lax.rem(lax.div(s, 4), 2)
        first = s + along_x * (1 - odd) + along_y * odd
        second = s + along_y * (1 - odd) + along_x * odd
        diagonal = s + along_x + along_y
        across = 1 - 2 * lax.rem(s, 2)
        pair = v + 1 - 2 * odd
        streams = [
            (s, (first, v), first),
            (first, (second, v), diagonal),
            (first, (s, pair), second),
            (s, (s + across, v), s + across),
            (first, (s + across, v), first + across),
            (diagonal, (s + across, v), diagonal + across),
            (second, (s + across, v), second + across),
        ]
    else:
        streams = [(s, (peer, v), source) for peer, source in zip(store_peers, store_from)]

    def send(t, k):
        origin, target, _ = streams[t]
        if origin is s:
            src = hidden.at[:, pl.ds(pl.multiple_of(k * KC, KC), KC)]
        else:
            src = hid.at[k, rows(origin)]
        return remote(src, hid.at[k, rows(origin)], gsend.at[t, k], grecv.at[t, k], *target)

    def arrive(t, k):
        _, target, origin = streams[t]
        block = hid.at[k, rows(origin)]
        return remote(block, block, gsend.at[t, k], grecv.at[t, k], *target)

    if tuned:
        loop_all(lambda k: send(0, k).start())
        loop_all(lambda k: send(3, k).start())
    else:
        for t in range(len(streams)):
            loop_all(lambda k: send(t, k).start())
    loop_all(lambda k: head_copy(k).start())

    for copy in small:
        copy.wait()
    tok[...] = jnp.broadcast_to(val[...], tok.shape)
    token_sends = []
    for j in range(1, V):
        copy = remote(tok, tokcol.at[v], tsend.at[j - 1], trecv.at[j - 1], s, vocab_peers[j - 1])
        copy.start()
        token_sends.append(copy)
    tokcol[v] = tok[...]

    logits[...] = jnp.zeros_like(logits)
    scores[...] = jnp.zeros_like(scores)
    half[...] = jnp.zeros_like(half)

    def norm_step(k, carry):
        key_copy(k).wait()
        wide = key[k].astype(jnp.float32)
        half[...] += jnp.sum(wide * wide, axis=1, keepdims=True)
        return carry

    lax.fori_loop(0, K, norm_step, 0)

    NT = math.gcd(C, COLUMN_CHUNK)

    def add_scores(k):
        own_copy(k).wait()
        scores[...] += lax.dot_general(
            key[k], hid[k], (((1,), (1,)), ((), ())), preferred_element_type=jnp.float32
        )

    def add_logits(k):
        head_copy(k).wait()

        def column_step(n, carry):
            cols = pl.ds(pl.multiple_of(n * NT, NT), NT)
            logits[:, cols] += jnp.dot(
                hid[k], head[k, :, cols], preferred_element_type=jnp.float32
            )
            return carry

        lax.fori_loop(0, C // NT, column_step, 0)

    def ready(k):
        for t in range(3, 7) if tuned else range(len(streams)):
            arrive(t, k).wait_recv()
        add_scores(k)

    def gather_step(k, carry):
        if tuned:
            @pl.when(k < K)
            def _():
                arrive(0, k).wait_recv()
                send(1, k).start()
                send(2, k).start()
                send(4, k).start()

        if tuned:
            @pl.when(jnp.logical_and(k >= 1, k <= K))
            def _():
                arrive(1, k - 1).wait_recv()
                send(5, k - 1).start()
                arrive(2, k - 1).wait_recv()
                send(6, k - 1).start()

        @pl.when(k >= lag)
        def _():
            ready(k - lag)
            add_logits(k - lag)

        return carry

    lag = 2 if tuned else 0
    lax.fori_loop(0, K - 1 + lag, gather_step, 0)
    ready(K - 1)

    licence = row_to_column(lic[...])[:, 0:1]
    permitted = jnp.bitwise_and(
        jnp.right_shift(
            jnp.broadcast_to(allow[...], (E, Q)), jnp.broadcast_to(licence, (E, Q))
        ), 1) == 1
    masked = jnp.where(
        permitted, scores[...] * inverse_root - (0.5 * inverse_root) * half[...], NEG_FILL
    )
    near = jnp.max(masked, axis=0, keepdims=True)
    kernel = jnp.where(permitted, jnp.exp(masked - near), 0.0)
    mass = jnp.sum(kernel, axis=0, keepdims=True)
    wsend[...] = kernel.astype(jnp.bfloat16)
    weight_sends = []
    for j in range(1, V):
        peer = vocab_peers[j - 1]
        copy = remote(
            wsend.at[pl.ds(pl.multiple_of(peer * B, B), B)], wrecv.at[v],
            wsend_sem.at[j - 1], wrecv_sem.at[j - 1], s, peer,
        )
        copy.start()
        weight_sends.append(copy)
    wrecv[v] = wsend[pl.ds(pl.multiple_of(v * B, B), B), :]

    add_logits(K - 1)
    out_copy = pltpu.make_async_copy(logits, logits_out, out_sem)
    out_copy.start()
    RT = math.gcd(Q, 64)
    lane = lax.broadcasted_iota(jnp.int32, (RT, 128), 1)

    def stat_step(r, carry):
        span = pl.ds(pl.multiple_of(r * RT, RT), RT)
        tile = logits[span, :]
        top = jnp.max(tile, axis=1, keepdims=True)
        total = jnp.sum(jnp.exp(tile - top), axis=1, keepdims=True)
        stat[span, :] = jnp.where(
            lane == 0, jnp.broadcast_to(top, (RT, 128)), jnp.broadcast_to(total, (RT, 128))
        )
        return carry

    lax.fori_loop(0, Q // RT, stat_step, 0)
    st1[0:2, :] = stat[...].T[0:2, :]
    st1[2:3, :] = near
    st1[3:4, :] = mass
    st1[4:8, :] = jnp.zeros((4, Q), jnp.float32)
    stat_sends = []
    for j in range(1, S):
        copy = remote(st1, st1_all.at[s], s1send.at[j - 1], s1recv.at[j - 1], store_peers[j - 1], v)
        copy.start()
        stat_sends.append(copy)
    st1_all[s] = st1[...]

    first_col = (s * V + v) * C
    for j in range(1, V):
        slot = tokcol.at[vocab_from[j - 1]]
        remote(slot, slot, tsend.at[j - 1], trecv.at[j - 1], s, vocab_peers[j - 1]).wait_recv()
    for u in range(V):
        turn[...] = row_to_column(tokcol[u, 0:1, :])
        tokens_out[u * B:(u + 1) * B, :] = turn[pl.ds(pl.multiple_of(v * B, B), B), :] - first_col

    def merge(ref, n):
        top = ref[0, 0:1, :]
        near_top = ref[0, 2:3, :]
        for i in range(1, n):
            top = jnp.maximum(top, ref[i, 0:1, :])
            near_top = jnp.maximum(near_top, ref[i, 2:3, :])
        total = jnp.zeros_like(top)
        near_total = jnp.zeros_like(top)
        for i in range(n):
            total += ref[i, 1:2, :] * jnp.exp(ref[i, 0:1, :] - top)
            near_total += ref[i, 3:4, :] * jnp.exp(ref[i, 2:3, :] - near_top)
        return top, total, near_top, near_total

    for j in range(1, S):
        slot = st1_all.at[store_from[j - 1]]
        remote(slot, slot, s1send.at[j - 1], s1recv.at[j - 1], store_peers[j - 1], v).wait_recv()
    for i, row in enumerate(merge(st1_all, S)):
        st2[i:i + 1, :] = row
    st2[4:5, :] = near
    st2[5:8, :] = jnp.zeros((3, Q), jnp.float32)
    for j in range(1, V):
        copy = remote(st2, st2_all.at[v], s2send.at[j - 1], s2recv.at[j - 1], s, vocab_peers[j - 1])
        copy.start()
        stat_sends.append(copy)
    st2_all[v] = st2[...]
    for j in range(1, V):
        source = vocab_from[j - 1]
        slot = st2_all.at[source]
        remote(slot, slot, s2send.at[j - 1], s2recv.at[j - 1], s, vocab_peers[j - 1]).wait_recv()
        slot = wrecv.at[source]
        remote(slot, slot, wsend_sem.at[j - 1], wrecv_sem.at[j - 1], s, vocab_peers[j - 1]).wait_recv()
    top, total, near_top, near_total = merge(st2_all, V)
    shift_out[...] = row_to_column(top + jnp.log(total) - math.log(0.75))
    for u in range(V):
        scale = 0.25 * jnp.exp(st2_all[u, 4:5, :] - near_top) / near_total
        weights_out[u * B:(u + 1) * B, :] = (wrecv[u].astype(jnp.float32) * scale).astype(jnp.bfloat16)

    if tuned:
        def drain(k):
            for t in range(len(streams)):
                send(t, k).wait_send()
        loop_all(drain)
    else:
        for t in range(len(streams)):
            loop_all(lambda k: send(t, k).wait_send())
    for copy in token_sends + weight_sends + stat_sends:
        copy.wait_send()
    out_copy.wait()


def mixture_kernel(weights, tokens, shift, logits, out):
    columns = lax.broadcasted_iota(jnp.int32, (tokens.shape[0], out.shape[1]), 1)
    columns += pl.program_id(0) * out.shape[1]
    table = jnp.where(tokens[:, 0:1] == columns, 1.0, 0.0).astype(jnp.bfloat16)
    share = lax.dot_general(
        weights[...], table, (((0,), (0,)), ((), ())), preferred_element_type=jnp.float32
    )
    ours = logits[...] - shift[:, 0:1]
    base = jnp.maximum(ours, -80.0)
    both = base + jnp.log(jnp.exp(ours - base) + share * jnp.exp(-base))
    out[...] = jnp.where(share > 0.0, both, ours)


def body(S, V, hidden, lm_head, keys, values, licences, allowed):
    R, D = hidden.shape
    C = lm_head.shape[1]
    E = keys.shape[0]
    Q = allowed.shape[0]
    B = E // V
    KC = math.gcd(D, DEPTH_CHUNK)
    K = D // KC
    streams = S - 1
    hbm = pl.BlockSpec(memory_space=pltpu.HBM)
    vmem = pl.BlockSpec(memory_space=pltpu.VMEM)
    f32 = jnp.float32
    dma = pltpu.SemaphoreType.DMA
    logits, weights, tokens, shift = pl.pallas_call(
        functools.partial(gather_kernel, S, V),
        out_shape=(
            jax.ShapeDtypeStruct((Q, C), f32),
            jax.ShapeDtypeStruct((E, Q), jnp.bfloat16),
            jax.ShapeDtypeStruct((E, 128), jnp.int32),
            jax.ShapeDtypeStruct((Q, 128), f32),
        ),
        in_specs=[hbm] * 6,
        out_specs=(hbm, vmem, vmem, vmem),
        scratch_shapes=[
            pltpu.VMEM((K, Q, KC), hidden.dtype),
            pltpu.VMEM((K, KC, C), lm_head.dtype),
            pltpu.VMEM((K, E, KC), keys.dtype),
            pltpu.VMEM((1, E), jnp.int32),
            pltpu.VMEM((1, Q), jnp.int32),
            pltpu.VMEM((1, E), jnp.int32),
            pltpu.VMEM((Q, C), f32),
            pltpu.VMEM((E, Q), f32),
            pltpu.VMEM((E, 1), f32),
            pltpu.VMEM((E, Q), jnp.bfloat16),
            pltpu.VMEM((V, B, Q), jnp.bfloat16),
            pltpu.VMEM((8, E), jnp.int32),
            pltpu.VMEM((V, 8, E), jnp.int32),
            pltpu.VMEM((E, 128), jnp.int32),
            pltpu.VMEM((Q, 128), f32),
            pltpu.VMEM((8, Q), f32),
            pltpu.VMEM((S, 8, Q), f32),
            pltpu.VMEM((8, Q), f32),
            pltpu.VMEM((V, 8, Q), f32),
            dma((K,)), dma((K,)), dma((K,)), dma((3,)), dma(()),
            dma((streams, K)), dma((streams, K)),
            dma((V - 1,)), dma((V - 1,)), dma((V - 1,)), dma((V - 1,)),
            dma((S - 1,)), dma((S - 1,)), dma((V - 1,)), dma((V - 1,)),
        ],
        compiler_params=pltpu.CompilerParams(
            collective_id=0, has_side_effects=True, vmem_limit_bytes=60 * 1024 * 1024
        ),
        name="gather_score",
    )(hidden, lm_head, keys, values.reshape(1, E), licences.reshape(1, E), allowed.reshape(1, Q))

    CT = math.gcd(C, COLUMN_CHUNK)
    fixed = lambda shape: pl.BlockSpec(shape, lambda n: (0, 0))
    tile = pl.BlockSpec((Q, CT), lambda n: (0, n))
    return pl.pallas_call(
        mixture_kernel,
        grid=(C // CT,),
        out_shape=jax.ShapeDtypeStruct((Q, C), f32),
        in_specs=[fixed((E, Q)), fixed((E, 128)), fixed((Q, 128)), tile],
        out_specs=tile,
        compiler_params=pltpu.CompilerParams(vmem_limit_bytes=60 * 1024 * 1024),
        name="mixture",
    )(weights, tokens, shift, logits)


def solution(mesh):
    return jax.shard_map(
        functools.partial(body, mesh.shape["store"], mesh.shape["vocab"]),
        mesh=mesh,
        in_specs=(
            P("store", None),
            P(None, ("store", "vocab")),
            P(("store", "vocab"), None),
            P(("store", "vocab")),
            P(("store", "vocab")),
            P(),
        ),
        out_specs=P(None, ("store", "vocab")),
        check_vma=False,
    )
```

```python
import functools
import math

import jax
import jax.numpy as jnp
from jax import lax
from jax.experimental import pallas as pl
from jax.experimental.pallas import tpu as pltpu
from jax.sharding import PartitionSpec as P

NEG_FILL = -1e30
DEPTH_CHUNK = 1024
COLUMN_CHUNK = 1024
MESH = pl.DeviceIdType.MESH


def row_to_column(row, lanes=128):
    return jnp.broadcast_to(row, (lanes, row.shape[1])).T


def gather_kernel(
    S, V,
    hidden, lm_head, keys, values, licences, allowed,
    logits_out, weights_out, tokens_out, shift_out,
    hid, head, key, lic, allow, val, logits, scores, half, wsend, wrecv, tok, tokcol, turn, stat, st1, st1_all, st2, st2_all,
    own_sem, head_sem, key_sem, small_sem, out_sem, gsend, grecv, tsend, trecv, wsend_sem, wrecv_sem,
    s1send, s1recv, s2send, s2recv,
):
    R, D = hidden.shape
    C = lm_head.shape[1]
    E = keys.shape[0]
    Q = hid.shape[1]
    K, KC = hid.shape[0], hid.shape[2]
    B = E // V
    inverse_root = 1.0 / math.sqrt(D)
    s = lax.axis_index("store")
    v = lax.axis_index("vocab")

    def rows(origin):
        return pl.ds(pl.multiple_of(origin * R, R), R)

    def remote(src, dst, send, recv, store, vocab):
        return pltpu.make_async_remote_copy(
            src_ref=src, dst_ref=dst, send_sem=send, recv_sem=recv,
            device_id=(store, vocab), device_id_type=MESH,
        )

    def own_copy(k):
        return pltpu.make_async_copy(
            hidden.at[:, pl.ds(pl.multiple_of(k * KC, KC), KC)], hid.at[k, rows(s)], own_sem.at[k]
        )

    def head_copy(k):
        return pltpu.make_async_copy(
            lm_head.at[pl.ds(pl.multiple_of(k * KC, KC), KC)], head.at[k], head_sem.at[k]
        )

    def key_copy(k):
        return pltpu.make_async_copy(
            keys.at[:, pl.ds(pl.multiple_of(k * KC, KC), KC)], key.at[k], key_sem.at[k]
        )

    def loop_all(f):
        def step(k, carry):
            f(k)
            return carry
        lax.fori_loop(0, K, step, 0)

    loop_all(lambda k: own_copy(k).start())
    loop_all(lambda k: key_copy(k).start())
    small = [
        pltpu.make_async_copy(src, dst, small_sem.at[i])
        for i, (src, dst) in enumerate(((values, val), (licences, lic), (allowed, allow)))
    ]
    for copy in small:
        copy.start()

    store_peers = [lax.rem(s + j, S) for j in range(1, S)]
    vocab_peers = [lax.rem(v + j, V) for j in range(1, V)]
    vocab_from = [lax.rem(v + V - j, V) for j in range(1, V)]
    store_from = [lax.rem(s + S - j, S) for j in range(1, S)]

    barrier = pltpu.get_barrier_semaphore()
    for peer in store_peers:
        pl.semaphore_signal(barrier, inc=1, device_id=(peer, v), device_id_type=MESH)
    for peer in vocab_peers:
        pl.semaphore_signal(barrier, inc=1, device_id=(s, peer), device_id_type=MESH)
    pl.semaphore_wait(barrier, S + V - 2)

    tuned = S == 8 and V % 2 == 0
    if tuned:
        odd = lax.rem(v, 2)
        along_x = 2 - 4 * lax.rem(lax.div(s, 2), 2)
        along_y = 4 - 8 * lax.rem(lax.div(s, 4), 2)
        first = s + along_x * (1 - odd) + along_y * odd
        second = s + along_y * (1 - odd) + along_x * odd
        diagonal = s + along_x + along_y
        across = 1 - 2 * lax.rem(s, 2)
        pair = v + 1 - 2 * odd
        streams = [
            (s, (first, v), first),
            (first, (second, v), diagonal),
            (first, (s, pair), second),
            (s, (s + across, v), s + across),
            (first, (s + across, v), first + across),
            (diagonal, (s + across, v), diagonal + across),
            (second, (s + across, v), second + across),
        ]
    else:
        streams = [(s, (peer, v), source) for peer, source in zip(store_peers, store_from)]

    def send(t, k):
        origin, target, _ = streams[t]
        src = hid.at[k, rows(origin)]
        return remote(src, hid.at[k, rows(origin)], gsend.at[t, k], grecv.at[t, k], *target)

    def arrive(t, k):
        _, target, origin = streams[t]
        block = hid.at[k, rows(origin)]
        return remote(block, block, gsend.at[t, k], grecv.at[t, k], *target)

    if tuned:
        def begin(k):
            own_copy(k).wait()
            send(0, k).start()
            send(3, k).start()
        loop_all(begin)
    else:
        loop_all(lambda k: own_copy(k).wait())
        for t in range(len(streams)):
            loop_all(lambda k: send(t, k).start())
    loop_all(lambda k: head_copy(k).start())

    for copy in small:
        copy.wait()
    tok[...] = jnp.broadcast_to(val[...], tok.shape)
    token_sends = []
    for j in range(1, V):
        copy = remote(tok, tokcol.at[v], tsend.at[j - 1], trecv.at[j - 1], s, vocab_peers[j - 1])
        copy.start()
        token_sends.append(copy)
    tokcol[v] = tok[...]

    logits[...] = jnp.zeros_like(logits)
    scores[...] = jnp.zeros_like(scores)
    half[...] = jnp.zeros_like(half)

    def norm_step(k, carry):
        key_copy(k).wait()
        wide = key[k].astype(jnp.float32)
        half[...] += jnp.sum(wide * wide, axis=1, keepdims=True)
        return carry

    lax.fori_loop(0, K, norm_step, 0)

    NT = math.gcd(C, 2 * COLUMN_CHUNK)

    def add_scores(k):
        scores[...] += lax.dot_general(
            key[k], hid[k], (((1,), (1,)), ((), ())), preferred_element_type=jnp.float32
        )

    def add_logits(k):
        head_copy(k).wait()

        def column_step(n, carry):
            cols = pl.ds(pl.multiple_of(n * NT, NT), NT)
            logits[:, cols] += jnp.dot(
                hid[k], head[k, :, cols], preferred_element_type=jnp.float32
            )
            return carry

        lax.fori_loop(0, C // NT, column_step, 0)

    def ready(k):
        for t in range(3, 7) if tuned else range(len(streams)):
            arrive(t, k).wait_recv()
        add_scores(k)

    def gather_step(k, carry):
        if tuned:
            @pl.when(k < K)
            def _():
                arrive(0, k).wait_recv()
                send(1, k).start()
                send(2, k).start()
                send(4, k).start()

        if tuned:
            @pl.when(jnp.logical_and(k >= 1, k <= K))
            def _():
                arrive(1, k - 1).wait_recv()
                send(5, k - 1).start()
                arrive(2, k - 1).wait_recv()
                send(6, k - 1).start()

        @pl.when(k >= lag)
        def _():
            ready(k - lag)
            add_logits(k - lag)

        return carry

    lag = 2 if tuned else 0
    lax.fori_loop(0, K - 1 + lag, gather_step, 0)
    ready(K - 1)

    licence = row_to_column(lic[...])[:, 0:1]
    permitted = jnp.bitwise_and(
        jnp.right_shift(
            jnp.broadcast_to(allow[...], (E, Q)), jnp.broadcast_to(licence, (E, Q))
        ), 1) == 1
    masked = jnp.where(
        permitted, scores[...] * inverse_root - (0.5 * inverse_root) * half[...], NEG_FILL
    )
    near = jnp.max(masked, axis=0, keepdims=True)
    kernel = jnp.where(permitted, jnp.exp(masked - near), 0.0)
    mass = jnp.sum(kernel, axis=0, keepdims=True)
    wsend[...] = kernel.astype(jnp.bfloat16)
    weight_sends = []
    for j in range(1, V):
        peer = vocab_peers[j - 1]
        copy = remote(
            wsend.at[pl.ds(pl.multiple_of(peer * B, B), B)], wrecv.at[v],
            wsend_sem.at[j - 1], wrecv_sem.at[j - 1], s, peer,
        )
        copy.start()
        weight_sends.append(copy)
    wrecv[v] = wsend[pl.ds(pl.multiple_of(v * B, B), B), :]

    add_logits(K - 1)
    out_copy = pltpu.make_async_copy(logits, logits_out, out_sem)
    out_copy.start()
    RT = math.gcd(Q, 64)
    lane = lax.broadcasted_iota(jnp.int32, (RT, 128), 1)

    def stat_step(r, carry):
        span = pl.ds(pl.multiple_of(r * RT, RT), RT)
        tile = logits[span, :]
        top = jnp.max(tile, axis=1, keepdims=True)
        total = jnp.sum(jnp.exp(tile - top), axis=1, keepdims=True)
        stat[span, :] = jnp.where(
            lane == 0, jnp.broadcast_to(top, (RT, 128)), jnp.broadcast_to(total, (RT, 128))
        )
        return carry

    lax.fori_loop(0, Q // RT, stat_step, 0)
    st1[0:2, :] = stat[...].T[0:2, :]
    st1[2:3, :] = near
    st1[3:4, :] = mass
    st1[4:8, :] = jnp.zeros((4, Q), jnp.float32)
    stat_sends = []
    for j in range(1, S):
        copy = remote(st1, st1_all.at[s], s1send.at[j - 1], s1recv.at[j - 1], store_peers[j - 1], v)
        copy.start()
        stat_sends.append(copy)
    st1_all[s] = st1[...]

    first_col = (s * V + v) * C
    for j in range(1, V):
        slot = tokcol.at[vocab_from[j - 1]]
        remote(slot, slot, tsend.at[j - 1], trecv.at[j - 1], s, vocab_peers[j - 1]).wait_recv()
    for u in range(V):
        turn[...] = row_to_column(tokcol[u, 0:1, :])
        tokens_out[u * B:(u + 1) * B, :] = turn[pl.ds(pl.multiple_of(v * B, B), B), :] - first_col

    def merge(ref, n):
        top = ref[0, 0:1, :]
        near_top = ref[0, 2:3, :]
        for i in range(1, n):
            top = jnp.maximum(top, ref[i, 0:1, :])
            near_top = jnp.maximum(near_top, ref[i, 2:3, :])
        total = jnp.zeros_like(top)
        near_total = jnp.zeros_like(top)
        for i in range(n):
            total += ref[i, 1:2, :] * jnp.exp(ref[i, 0:1, :] - top)
            near_total += ref[i, 3:4, :] * jnp.exp(ref[i, 2:3, :] - near_top)
        return top, total, near_top, near_total

    for j in range(1, S):
        slot = st1_all.at[store_from[j - 1]]
        remote(slot, slot, s1send.at[j - 1], s1recv.at[j - 1], store_peers[j - 1], v).wait_recv()
    for i, row in enumerate(merge(st1_all, S)):
        st2[i:i + 1, :] = row
    st2[4:5, :] = near
    st2[5:8, :] = jnp.zeros((3, Q), jnp.float32)
    for j in range(1, V):
        copy = remote(st2, st2_all.at[v], s2send.at[j - 1], s2recv.at[j - 1], s, vocab_peers[j - 1])
        copy.start()
        stat_sends.append(copy)
    st2_all[v] = st2[...]
    for j in range(1, V):
        source = vocab_from[j - 1]
        slot = st2_all.at[source]
        remote(slot, slot, s2send.at[j - 1], s2recv.at[j - 1], s, vocab_peers[j - 1]).wait_recv()
        slot = wrecv.at[source]
        remote(slot, slot, wsend_sem.at[j - 1], wrecv_sem.at[j - 1], s, vocab_peers[j - 1]).wait_recv()
    top, total, near_top, near_total = merge(st2_all, V)
    shift_out[...] = row_to_column(top + jnp.log(total) - math.log(0.75))
    for u in range(V):
        scale = 0.25 * jnp.exp(st2_all[u, 4:5, :] - near_top) / near_total
        weights_out[u * B:(u + 1) * B, :] = (wrecv[u].astype(jnp.float32) * scale).astype(jnp.bfloat16)

    if tuned:
        def drain(k):
            for t in range(len(streams)):
                send(t, k).wait_send()
        loop_all(drain)
    else:
        for t in range(len(streams)):
            loop_all(lambda k: send(t, k).wait_send())
    for copy in token_sends + weight_sends + stat_sends:
        copy.wait_send()
    out_copy.wait()


def mixture_kernel(weights, tokens, shift, logits, out):
    columns = lax.broadcasted_iota(jnp.int32, (tokens.shape[0], out.shape[1]), 1)
    columns += pl.program_id(0) * out.shape[1]
    table = jnp.where(tokens[:, 0:1] == columns, 1.0, 0.0).astype(jnp.bfloat16)
    share = lax.dot_general(
        weights[...], table, (((0,), (0,)), ((), ())), preferred_element_type=jnp.float32
    )
    ours = logits[...] - shift[:, 0:1]
    base = jnp.maximum(ours, -80.0)
    both = base + jnp.log(jnp.exp(ours - base) + share * jnp.exp(-base))
    out[...] = jnp.where(share > 0.0, both, ours)


def body(S, V, hidden, lm_head, keys, values, licences, allowed):
    R, D = hidden.shape
    C = lm_head.shape[1]
    E = keys.shape[0]
    Q = allowed.shape[0]
    B = E // V
    KC = math.gcd(D, DEPTH_CHUNK)
    K = D // KC
    streams = S - 1
    hbm = pl.BlockSpec(memory_space=pltpu.HBM)
    vmem = pl.BlockSpec(memory_space=pltpu.VMEM)
    f32 = jnp.float32
    dma = pltpu.SemaphoreType.DMA
    logits, weights, tokens, shift = pl.pallas_call(
        functools.partial(gather_kernel, S, V),
        out_shape=(
            jax.ShapeDtypeStruct((Q, C), f32),
            jax.ShapeDtypeStruct((E, Q), jnp.bfloat16),
            jax.ShapeDtypeStruct((E, 128), jnp.int32),
            jax.ShapeDtypeStruct((Q, 128), f32),
        ),
        in_specs=[hbm] * 6,
        out_specs=(hbm, vmem, vmem, vmem),
        scratch_shapes=[
            pltpu.VMEM((K, Q, KC), hidden.dtype),
            pltpu.VMEM((K, KC, C), lm_head.dtype),
            pltpu.VMEM((K, E, KC), keys.dtype),
            pltpu.VMEM((1, E), jnp.int32),
            pltpu.VMEM((1, Q), jnp.int32),
            pltpu.VMEM((1, E), jnp.int32),
            pltpu.VMEM((Q, C), f32),
            pltpu.VMEM((E, Q), f32),
            pltpu.VMEM((E, 1), f32),
            pltpu.VMEM((E, Q), jnp.bfloat16),
            pltpu.VMEM((V, B, Q), jnp.bfloat16),
            pltpu.VMEM((8, E), jnp.int32),
            pltpu.VMEM((V, 8, E), jnp.int32),
            pltpu.VMEM((E, 128), jnp.int32),
            pltpu.VMEM((Q, 128), f32),
            pltpu.VMEM((8, Q), f32),
            pltpu.VMEM((S, 8, Q), f32),
            pltpu.VMEM((8, Q), f32),
            pltpu.VMEM((V, 8, Q), f32),
            dma((K,)), dma((K,)), dma((K,)), dma((3,)), dma(()),
            dma((streams, K)), dma((streams, K)),
            dma((V - 1,)), dma((V - 1,)), dma((V - 1,)), dma((V - 1,)),
            dma((S - 1,)), dma((S - 1,)), dma((V - 1,)), dma((V - 1,)),
        ],
        compiler_params=pltpu.CompilerParams(
            collective_id=0, has_side_effects=True, vmem_limit_bytes=60 * 1024 * 1024
        ),
        name="gather_score",
    )(hidden, lm_head, keys, values.reshape(1, E), licences.reshape(1, E), allowed.reshape(1, Q))

    CT = math.gcd(C, COLUMN_CHUNK)
    fixed = lambda shape: pl.BlockSpec(shape, lambda n: (0, 0))
    tile = pl.BlockSpec((Q, CT), lambda n: (0, n))
    return pl.pallas_call(
        mixture_kernel,
        grid=(C // CT,),
        out_shape=jax.ShapeDtypeStruct((Q, C), f32),
        in_specs=[fixed((E, Q)), fixed((E, 128)), fixed((Q, 128)), tile],
        out_specs=tile,
        compiler_params=pltpu.CompilerParams(vmem_limit_bytes=60 * 1024 * 1024),
        name="mixture",
    )(weights, tokens, shift, logits)


def solution(mesh):
    return jax.shard_map(
        functools.partial(body, mesh.shape["store"], mesh.shape["vocab"]),
        mesh=mesh,
        in_specs=(
            P("store", None),
            P(None, ("store", "vocab")),
            P(("store", "vocab"), None),
            P(("store", "vocab")),
            P(("store", "vocab")),
            P(),
        ),
        out_specs=P(None, ("store", "vocab")),
        check_vma=False,
    )
```

```python
import functools
import math

import jax
import jax.numpy as jnp
from jax import lax
from jax.experimental import pallas as pl
from jax.experimental.pallas import tpu as pltpu
from jax.sharding import PartitionSpec as P

NEG_FILL = -1e30
DEPTH_CHUNK = 1024
COLUMN_CHUNK = 1024
MESH = pl.DeviceIdType.MESH


def row_to_column(row, lanes=128):
    return jnp.broadcast_to(row, (lanes, row.shape[1])).T


def gather_kernel(
    S, V,
    hidden, lm_head, keys, values, licences, allowed,
    logits_out, weights_out, tokens_out, shift_out,
    hid, head, key, lic, allow, val, logits, scores, half, wsend, wrecv, tok, tokcol, turn, stat, st1, st1_all, st2, st2_all,
    own_sem, head_sem, key_sem, small_sem, out_sem, gsend, grecv, tsend, trecv, wsend_sem, wrecv_sem,
    s1send, s1recv, s2send, s2recv,
):
    R, D = hidden.shape
    C = lm_head.shape[1]
    E = keys.shape[0]
    Q = hid.shape[1]
    K, KC = hid.shape[0], hid.shape[2]
    B = E // V
    inverse_root = 1.0 / math.sqrt(D)
    s = lax.axis_index("store")
    v = lax.axis_index("vocab")

    def rows(origin):
        return pl.ds(pl.multiple_of(origin * R, R), R)

    def remote(src, dst, send, recv, store, vocab):
        return pltpu.make_async_remote_copy(
            src_ref=src, dst_ref=dst, send_sem=send, recv_sem=recv,
            device_id=(store, vocab), device_id_type=MESH,
        )

    def own_copy(k):
        return pltpu.make_async_copy(
            hidden.at[:, pl.ds(pl.multiple_of(k * KC, KC), KC)], hid.at[k, rows(s)], own_sem.at[k]
        )

    def head_copy(k):
        return pltpu.make_async_copy(
            lm_head.at[pl.ds(pl.multiple_of(k * KC, KC), KC)], head.at[k], head_sem.at[k]
        )

    def key_copy(k):
        return pltpu.make_async_copy(
            keys.at[:, pl.ds(pl.multiple_of(k * KC, KC), KC)], key.at[k], key_sem.at[k]
        )

    def loop_all(f):
        def step(k, carry):
            f(k)
            return carry
        lax.fori_loop(0, K, step, 0)

    loop_all(lambda k: own_copy(k).start())
    loop_all(lambda k: key_copy(k).start())
    small = [
        pltpu.make_async_copy(src, dst, small_sem.at[i])
        for i, (src, dst) in enumerate(((values, val), (licences, lic), (allowed, allow)))
    ]
    for copy in small:
        copy.start()

    store_peers = [lax.rem(s + j, S) for j in range(1, S)]
    vocab_peers = [lax.rem(v + j, V) for j in range(1, V)]
    vocab_from = [lax.rem(v + V - j, V) for j in range(1, V)]
    store_from = [lax.rem(s + S - j, S) for j in range(1, S)]

    barrier = pltpu.get_barrier_semaphore()
    for peer in store_peers:
        pl.semaphore_signal(barrier, inc=1, device_id=(peer, v), device_id_type=MESH)
    for peer in vocab_peers:
        pl.semaphore_signal(barrier, inc=1, device_id=(s, peer), device_id_type=MESH)
    pl.semaphore_wait(barrier, S + V - 2)

    tuned = S == 8 and V % 2 == 0
    if tuned:
        odd = lax.rem(v, 2)
        along_x = 2 - 4 * lax.rem(lax.div(s, 2), 2)
        along_y = 4 - 8 * lax.rem(lax.div(s, 4), 2)
        first = s + along_x * (1 - odd) + along_y * odd
        second = s + along_y * (1 - odd) + along_x * odd
        diagonal = s + along_x + along_y
        across = 1 - 2 * lax.rem(s, 2)
        pair = v + 1 - 2 * odd
        streams = [
            (s, (first, v), first),
            (first, (second, v), diagonal),
            (first, (s, pair), second),
            (s, (s + across, v), s + across),
            (first, (s + across, v), first + across),
            (diagonal, (s + across, v), diagonal + across),
            (second, (s + across, v), second + across),
        ]
    else:
        streams = [(s, (peer, v), source) for peer, source in zip(store_peers, store_from)]

    def send(t, k):
        origin, target, _ = streams[t]
        src = hid.at[k, rows(origin)]
        return remote(src, hid.at[k, rows(origin)], gsend.at[t, k], grecv.at[t, k], *target)

    def arrive(t, k):
        _, target, origin = streams[t]
        block = hid.at[k, rows(origin)]
        return remote(block, block, gsend.at[t, k], grecv.at[t, k], *target)

    if tuned:
        def begin(k):
            own_copy(k).wait()
            send(0, k).start()
            send(3, k).start()
        loop_all(begin)
    else:
        loop_all(lambda k: own_copy(k).wait())
        for t in range(len(streams)):
            loop_all(lambda k: send(t, k).start())
    loop_all(lambda k: head_copy(k).start())

    for copy in small:
        copy.wait()
    tok[...] = jnp.broadcast_to(val[...], tok.shape)
    token_sends = []
    for j in range(1, V):
        copy = remote(tok, tokcol.at[v], tsend.at[j - 1], trecv.at[j - 1], s, vocab_peers[j - 1])
        copy.start()
        token_sends.append(copy)
    tokcol[v] = tok[...]

    logits[...] = jnp.zeros_like(logits)
    scores[...] = jnp.zeros_like(scores)
    half[...] = jnp.zeros_like(half)

    def norm_step(k, carry):
        key_copy(k).wait()
        wide = key[k].astype(jnp.float32)
        half[...] += jnp.sum(wide * wide, axis=1, keepdims=True)
        return carry

    lax.fori_loop(0, K, norm_step, 0)

    NT = math.gcd(C, 2 * COLUMN_CHUNK)

    def add_scores(k):
        scores[...] += lax.dot_general(
            key[k], hid[k], (((1,), (1,)), ((), ())), preferred_element_type=jnp.float32
        )

    def add_logits(k):
        head_copy(k).wait()

        def column_step(n, carry):
            cols = pl.ds(pl.multiple_of(n * NT, NT), NT)
            logits[:, cols] += jnp.dot(
                hid[k], head[k, :, cols], preferred_element_type=jnp.float32
            )
            return carry

        lax.fori_loop(0, C // NT, column_step, 0)

    def ready(k):
        for t in range(3, 7) if tuned else range(len(streams)):
            arrive(t, k).wait_recv()
        add_scores(k)

    def gather_step(k, carry):
        if tuned:
            @pl.when(k < K)
            def _():
                arrive(0, k).wait_recv()
                send(1, k).start()
                send(2, k).start()
                send(4, k).start()

        if tuned:
            @pl.when(jnp.logical_and(k >= 1, k <= K))
            def _():
                arrive(1, k - 1).wait_recv()
                send(5, k - 1).start()
                arrive(2, k - 1).wait_recv()
                send(6, k - 1).start()

        @pl.when(k >= lag)
        def _():
            ready(k - lag)
            add_logits(k - lag)

        return carry

    lag = 2 if tuned else 0
    lax.fori_loop(0, K - 1 + lag, gather_step, 0)
    ready(K - 1)

    licence = row_to_column(lic[...])[:, 0:1]
    permitted = jnp.bitwise_and(
        jnp.right_shift(
            jnp.broadcast_to(allow[...], (E, Q)), jnp.broadcast_to(licence, (E, Q))
        ), 1) == 1
    masked = jnp.where(
        permitted, scores[...] * inverse_root - (0.5 * inverse_root) * half[...], NEG_FILL
    )
    near = jnp.max(masked, axis=0, keepdims=True)
    kernel = jnp.where(permitted, jnp.exp(masked - near), 0.0)
    mass = jnp.sum(kernel, axis=0, keepdims=True)
    wsend[...] = kernel.astype(jnp.bfloat16)
    weight_sends = []
    for j in range(1, V):
        peer = vocab_peers[j - 1]
        copy = remote(
            wsend.at[pl.ds(pl.multiple_of(peer * B, B), B)], wrecv.at[v],
            wsend_sem.at[j - 1], wrecv_sem.at[j - 1], s, peer,
        )
        copy.start()
        weight_sends.append(copy)
    wrecv[v] = wsend[pl.ds(pl.multiple_of(v * B, B), B), :]

    add_logits(K - 1)
    out_copy = pltpu.make_async_copy(logits, logits_out, out_sem)
    out_copy.start()
    RT = math.gcd(Q, 128)
    lane = lax.broadcasted_iota(jnp.int32, (RT, 128), 1)

    def stat_step(r, carry):
        span = pl.ds(pl.multiple_of(r * RT, RT), RT)
        tile = logits[span, :]
        top = jnp.max(tile, axis=1, keepdims=True)
        total = jnp.sum(jnp.exp(tile - top), axis=1, keepdims=True)
        stat[span, :] = jnp.where(
            lane == 0, jnp.broadcast_to(top, (RT, 128)), jnp.broadcast_to(total, (RT, 128))
        )
        return carry

    lax.fori_loop(0, Q // RT, stat_step, 0)
    st1[0:2, :] = stat[...].T[0:2, :]
    st1[2:3, :] = near
    st1[3:4, :] = mass
    st1[4:8, :] = jnp.zeros((4, Q), jnp.float32)
    stat_sends = []
    for j in range(1, S):
        copy = remote(st1, st1_all.at[s], s1send.at[j - 1], s1recv.at[j - 1], store_peers[j - 1], v)
        copy.start()
        stat_sends.append(copy)
    st1_all[s] = st1[...]

    first_col = (s * V + v) * C
    for j in range(1, V):
        slot = tokcol.at[vocab_from[j - 1]]
        remote(slot, slot, tsend.at[j - 1], trecv.at[j - 1], s, vocab_peers[j - 1]).wait_recv()
    for u in range(V):
        turn[...] = row_to_column(tokcol[u, 0:1, :])
        tokens_out[u * B:(u + 1) * B, :] = turn[pl.ds(pl.multiple_of(v * B, B), B), :] - first_col

    def merge(ref, n):
        top = ref[0, 0:1, :]
        near_top = ref[0, 2:3, :]
        for i in range(1, n):
            top = jnp.maximum(top, ref[i, 0:1, :])
            near_top = jnp.maximum(near_top, ref[i, 2:3, :])
        total = jnp.zeros_like(top)
        near_total = jnp.zeros_like(top)
        for i in range(n):
            total += ref[i, 1:2, :] * jnp.exp(ref[i, 0:1, :] - top)
            near_total += ref[i, 3:4, :] * jnp.exp(ref[i, 2:3, :] - near_top)
        return top, total, near_top, near_total

    for j in range(1, S):
        slot = st1_all.at[store_from[j - 1]]
        remote(slot, slot, s1send.at[j - 1], s1recv.at[j - 1], store_peers[j - 1], v).wait_recv()
    for i, row in enumerate(merge(st1_all, S)):
        st2[i:i + 1, :] = row
    st2[4:5, :] = near
    st2[5:8, :] = jnp.zeros((3, Q), jnp.float32)
    for j in range(1, V):
        copy = remote(st2, st2_all.at[v], s2send.at[j - 1], s2recv.at[j - 1], s, vocab_peers[j - 1])
        copy.start()
        stat_sends.append(copy)
    st2_all[v] = st2[...]
    for j in range(1, V):
        source = vocab_from[j - 1]
        slot = st2_all.at[source]
        remote(slot, slot, s2send.at[j - 1], s2recv.at[j - 1], s, vocab_peers[j - 1]).wait_recv()
        slot = wrecv.at[source]
        remote(slot, slot, wsend_sem.at[j - 1], wrecv_sem.at[j - 1], s, vocab_peers[j - 1]).wait_recv()
    top, total, near_top, near_total = merge(st2_all, V)
    shift_out[...] = row_to_column(top + jnp.log(total) - math.log(0.75))
    for u in range(V):
        scale = 0.25 * jnp.exp(st2_all[u, 4:5, :] - near_top) / near_total
        weights_out[u * B:(u + 1) * B, :] = (wrecv[u].astype(jnp.float32) * scale).astype(jnp.bfloat16)

    if tuned:
        def drain(k):
            for t in range(len(streams)):
                send(t, k).wait_send()
        loop_all(drain)
    else:
        for t in range(len(streams)):
            loop_all(lambda k: send(t, k).wait_send())
    for copy in token_sends + weight_sends + stat_sends:
        copy.wait_send()
    out_copy.wait()


def mixture_kernel(weights, tokens, shift, logits, out):
    columns = lax.broadcasted_iota(jnp.int32, (tokens.shape[0], out.shape[1]), 1)
    columns += pl.program_id(0) * out.shape[1]
    table = jnp.where(tokens[:, 0:1] == columns, 1.0, 0.0).astype(jnp.bfloat16)
    share = lax.dot_general(
        weights[...], table, (((0,), (0,)), ((), ())), preferred_element_type=jnp.float32
    )
    ours = logits[...] - shift[:, 0:1]
    base = jnp.maximum(ours, -80.0)
    both = base + jnp.log(jnp.exp(ours - base) + share * jnp.exp(-base))
    out[...] = jnp.where(share > 0.0, both, ours)


def body(S, V, hidden, lm_head, keys, values, licences, allowed):
    R, D = hidden.shape
    C = lm_head.shape[1]
    E = keys.shape[0]
    Q = allowed.shape[0]
    B = E // V
    KC = math.gcd(D, DEPTH_CHUNK)
    K = D // KC
    streams = S - 1
    hbm = pl.BlockSpec(memory_space=pltpu.HBM)
    vmem = pl.BlockSpec(memory_space=pltpu.VMEM)
    f32 = jnp.float32
    dma = pltpu.SemaphoreType.DMA
    logits, weights, tokens, shift = pl.pallas_call(
        functools.partial(gather_kernel, S, V),
        out_shape=(
            jax.ShapeDtypeStruct((Q, C), f32),
            jax.ShapeDtypeStruct((E, Q), jnp.bfloat16),
            jax.ShapeDtypeStruct((E, 128), jnp.int32),
            jax.ShapeDtypeStruct((Q, 128), f32),
        ),
        in_specs=[hbm] * 6,
        out_specs=(hbm, vmem, vmem, vmem),
        scratch_shapes=[
            pltpu.VMEM((K, Q, KC), hidden.dtype),
            pltpu.VMEM((K, KC, C), lm_head.dtype),
            pltpu.VMEM((K, E, KC), keys.dtype),
            pltpu.VMEM((1, E), jnp.int32),
            pltpu.VMEM((1, Q), jnp.int32),
            pltpu.VMEM((1, E), jnp.int32),
            pltpu.VMEM((Q, C), f32),
            pltpu.VMEM((E, Q), f32),
            pltpu.VMEM((E, 1), f32),
            pltpu.VMEM((E, Q), jnp.bfloat16),
            pltpu.VMEM((V, B, Q), jnp.bfloat16),
            pltpu.VMEM((8, E), jnp.int32),
            pltpu.VMEM((V, 8, E), jnp.int32),
            pltpu.VMEM((E, 128), jnp.int32),
            pltpu.VMEM((Q, 128), f32),
            pltpu.VMEM((8, Q), f32),
            pltpu.VMEM((S, 8, Q), f32),
            pltpu.VMEM((8, Q), f32),
            pltpu.VMEM((V, 8, Q), f32),
            dma((K,)), dma((K,)), dma((K,)), dma((3,)), dma(()),
            dma((streams, K)), dma((streams, K)),
            dma((V - 1,)), dma((V - 1,)), dma((V - 1,)), dma((V - 1,)),
            dma((S - 1,)), dma((S - 1,)), dma((V - 1,)), dma((V - 1,)),
        ],
        compiler_params=pltpu.CompilerParams(
            collective_id=0, has_side_effects=True, vmem_limit_bytes=60 * 1024 * 1024
        ),
        name="gather_score",
    )(hidden, lm_head, keys, values.reshape(1, E), licences.reshape(1, E), allowed.reshape(1, Q))

    CT = math.gcd(C, COLUMN_CHUNK)
    fixed = lambda shape: pl.BlockSpec(shape, lambda n: (0, 0))
    tile = pl.BlockSpec((Q, CT), lambda n: (0, n))
    return pl.pallas_call(
        mixture_kernel,
        grid=(C // CT,),
        out_shape=jax.ShapeDtypeStruct((Q, C), f32),
        in_specs=[fixed((E, Q)), fixed((E, 128)), fixed((Q, 128)), tile],
        out_specs=tile,
        compiler_params=pltpu.CompilerParams(vmem_limit_bytes=60 * 1024 * 1024),
        name="mixture",
    )(weights, tokens, shift, logits)


def solution(mesh):
    return jax.shard_map(
        functools.partial(body, mesh.shape["store"], mesh.shape["vocab"]),
        mesh=mesh,
        in_specs=(
            P("store", None),
            P(None, ("store", "vocab")),
            P(("store", "vocab"), None),
            P(("store", "vocab")),
            P(("store", "vocab")),
            P(),
        ),
        out_specs=P(None, ("store", "vocab")),
        check_vma=False,
    )
```
